32 devices in a mesh: rep: 4 (over y, x), grp: 2 (over core), exp: 4 (over z).
Axes of the slice: x: 2, y: 2, z: 4, core: 2. Of those that a mesh axis runs over, the one named last changes fastest.
Arguments:
- tokens: bfloat16 [4096, 2048], P(('rep', 'grp', 'exp')), may hold values from -6 to 6
- out_grad: bfloat16 [4096, 2048], P(('rep', 'grp', 'exp')), may hold values from -2.390625 to 2.390625
- routes: int32 [4096, 4], P(('rep', 'grp', 'exp')), may hold values from 0 to 7, as said below
- route_probs: bfloat16 [4096, 4], P(('rep', 'grp', 'exp')), may hold values from 0.049804688 to 0.59765625
- w_gate: bfloat16 [8, 2048, 768], P(('grp', 'exp')), may hold values from -0.125 to 0.125
- w_up: bfloat16 [8, 2048, 768], P(('grp', 'exp')), may hold values from -0.125 to 0.125
- w_down: bfloat16 [8, 768, 2048], P(('grp', 'exp')), may hold values from -0.21875 to 0.21875
Outputs:
- grad_tokens: bfloat16 [4096, 2048], P(('rep', 'grp', 'exp'))
- grad_probs: bfloat16 [4096, 4], P(('rep', 'grp', 'exp'))
- grad_gate: bfloat16 [8, 2048, 768], P(('grp', 'exp'), 'rep')
- grad_up: bfloat16 [8, 2048, 768], P(('grp', 'exp'), 'rep')
- grad_down: bfloat16 [8, 768, 2048], P(('grp', 'exp'), 'rep')
The draws below stay inside these ranges and needn't reach their ends.
Inputs may be any that keep to these rules, and one draw needn't show every extreme that they name: `routes`: each row names 4 different experts, all of one group (group g holds experts g * 4 to g * 4 + 3). In the rows of one device exactly 112 rows name one common group, the same for every device; the other rows name other groups. The slots that the rows of one device give to one group are spread over its experts as evenly as possible: no device names one expert in more than 112 rows, and every expert of the common group is named by exactly 112 rows of every device.
All inputs are finite; a program needn't handle non-finite values.
Results may differ from the reference program's by a relative error of at most 0.009.
Values may be sent and summed in bfloat16 or wider, within the bound.
A program may use at most 128 MiB of HBM per device.

```python
import jax
import jax.numpy as jnp
from jax import lax

D = 2048
FF = 768
TOK_DEV = 128
TOPK = 4
REPLICAS = 4
GROUPS = 2
GROUP_EXP = 4
EXPERTS = 8
HOT_ROWS = 112
TOKENS = 4096


def draw_routes(key, part):
    base_key = jax.random.fold_in(key, 7)
    hot_key, shuffle_key, cold_key, perm_key = jax.random.split(base_key, 4)
    blocks = TOKENS // TOK_DEV
    hot_group = jax.random.randint(hot_key, (), 0, GROUPS)
    shuffle = jax.vmap(lambda sub_key: jax.random.permutation(sub_key, TOK_DEV))(jax.random.split(shuffle_key, blocks))
    placed_at = jnp.argsort(shuffle, axis=1)
    cold_pick = jax.random.randint(cold_key, (blocks, TOK_DEV), 0, GROUPS - 1)
    group_of = jnp.where(placed_at < HOT_ROWS, hot_group, (hot_group + 1 + cold_pick) % GROUPS)
    placed_group = jnp.take_along_axis(group_of, shuffle, axis=1)
    members = (placed_group[:, :, None] == jnp.arange(GROUPS)[None, None, :]).astype(jnp.int32)
    earlier = jnp.cumsum(members, axis=1) - members
    placed_rank = jnp.sum(earlier * members, axis=2)
    rank_in = jnp.take_along_axis(placed_rank, placed_at, axis=1)
    within = (rank_in[:, :, None] * TOPK + jnp.arange(TOPK)[None, None, :]) % GROUP_EXP
    shuffles = jax.vmap(lambda sub_key: jax.random.permutation(sub_key, GROUP_EXP))(jax.random.split(perm_key, blocks * GROUPS)).reshape(blocks, GROUPS, GROUP_EXP)
    block_ids = jnp.arange(blocks)[:, None, None]
    local_ids = shuffles[block_ids, group_of[:, :, None], within]
    experts = group_of[:, :, None] * GROUP_EXP + local_ids
    return experts.reshape(TOKENS, TOPK).astype(jnp.int32)


def shard_levels(rng, dims, cuts, least, largest):
    def one(axis_at, blocks):
        draws = jax.random.uniform(jax.random.fold_in(jax.random.fold_in(rng, 6), axis_at), (blocks,), jnp.float32, least / len(cuts), largest / len(cuts))
        return jnp.repeat(jnp.exp(draws), dims[axis_at] // blocks).reshape((-1,) + (1,) * (len(dims) - axis_at - 1))

    gain = one(*cuts[0])
    for cut in cuts[1:]:
        gain = gain * one(*cut)
    return gain


def scatter_about(own_key, dims, scale, limit, shards=(), kind=jnp.bfloat16):
    factor_of = shard_levels(own_key, dims, shards, -0.22, 0.18) if shards else 1.0
    drawn = jax.random.normal(own_key, dims, jnp.float32) * scale * factor_of
    return jnp.minimum(jnp.maximum(drawn, -limit), limit).astype(kind)


def setup_inputs(seed: int = 0) -> dict:
    key_list = jax.random.split(jax.random.key(seed), 8)
    tokens = scatter_about(key_list[0], (TOKENS, D), 1.0, 6.0, ((0, 32),))
    out_grad = scatter_about(key_list[1], (TOKENS, D), 0.4, 2.390625, ((0, 32),))
    routes = draw_routes(jax.random.fold_in(key_list[7], 71), 0)
    route_probs = jnp.clip(0.049804688 + 0.54785156 * jax.random.uniform(key_list[3], (TOKENS, TOPK), jnp.float32) ** shard_levels(key_list[3], (TOKENS, TOPK), ((0, 32),), -0.2, 0.2), 0.049804688, 0.59765625).astype(jnp.bfloat16)
    w_gate = scatter_about(key_list[4], (EXPERTS, D, FF), D ** -0.5, 0.125, ((0, 8),))
    w_up = scatter_about(key_list[5], (EXPERTS, D, FF), D ** -0.5, 0.125, ((0, 8),))
    w_down = scatter_about(key_list[6], (EXPERTS, FF, D), FF ** -0.5, 0.21875, ((0, 8),))
    return dict(tokens=tokens, out_grad=out_grad, routes=routes, route_probs=route_probs, w_gate=w_gate, w_up=w_up, w_down=w_down)


def contract_rows(left, right):
    return lax.dot_general(left, right, (((0,), (0,)), ((), ())), preferred_element_type=jnp.float32)


def contract_cols(left, right):
    return lax.dot_general(left, right, (((1,), (1,)), ((), ())), preferred_element_type=jnp.float32)


def slot_backward(row_tokens, row_grads, row_probs, gate_mat, up_mat, down_mat):
    gate = jnp.dot(row_tokens, gate_mat, preferred_element_type=jnp.float32)
    up_value = jnp.dot(row_tokens, up_mat, preferred_element_type=jnp.float32)
    sigmoid_g = jax.nn.sigmoid(gate)
    active = gate * sigmoid_g
    hidden = (active * up_value).astype(jnp.bfloat16)
    expert_out = jnp.dot(hidden, down_mat, preferred_element_type=jnp.float32).astype(jnp.bfloat16)
    prob_grad = jnp.sum(row_grads.astype(jnp.float32) * expert_out.astype(jnp.float32), axis=1)
    slot_grad = (row_probs.astype(jnp.float32)[:, None] * row_grads.astype(jnp.float32)).astype(jnp.bfloat16)
    grad_hidden = contract_cols(slot_grad, down_mat)
    pre_gate = (grad_hidden * up_value * sigmoid_g * (1.0 + gate * (1.0 - sigmoid_g))).astype(jnp.bfloat16)
    pre_up = (grad_hidden * active).astype(jnp.bfloat16)
    slot_input = (contract_cols(pre_gate, gate_mat) + contract_cols(pre_up, up_mat)).astype(jnp.bfloat16)
    return slot_input, prob_grad, hidden, slot_grad, pre_gate, pre_up


def reference(tokens, out_grad, routes, route_probs, w_gate, w_up, w_down):
    slot_count = TOKENS * TOPK
    block_rows = 128
    slot_expert = routes.reshape(-1).astype(jnp.int32)
    slot_token = (jnp.arange(slot_count, dtype=jnp.int32) // TOPK).astype(jnp.int32)
    slot_replica = (slot_token // (TOK_DEV * GROUPS * GROUP_EXP)).astype(jnp.int32)
    group_key = (slot_expert * REPLICAS + slot_replica).astype(jnp.int32)
    sorted_slots = jnp.argsort(group_key, stable=True).astype(jnp.int32)
    counts = jnp.zeros((EXPERTS * REPLICAS,), jnp.int32).at[group_key].add(1)
    starts = (jnp.cumsum(counts) - counts).astype(jnp.int32)
    padded_slots = jnp.concatenate([sorted_slots, jnp.zeros((block_rows,), jnp.int32)])
    probs_flat = route_probs.reshape(-1)

    def expert_step(expert, carry):
        grad_acc, prob_out, gate_out, up_out, down_out = carry
        gate_mat = w_gate[expert]
        up_mat = w_up[expert]
        down_mat = w_down[expert]

        def replica_step(replica, inner):
            grad_acc, prob_out, sum_gate, sum_up, sum_down = inner
            which = (expert * REPLICAS + replica).astype(jnp.int32)
            live_rows = counts[which]
            first_row = starts[which]

            def block_step(step_no, state):
                grad_acc, prob_out, part_gate, part_up, part_down = state
                offset = (first_row + step_no * block_rows).astype(jnp.int32)
                slot_ids = lax.dynamic_slice_in_dim(padded_slots, offset, block_rows)
                is_live = (jnp.arange(block_rows, dtype=jnp.int32) + step_no * block_rows) < live_rows
                token_ids = slot_token[slot_ids]
                row_tokens = jnp.where(is_live[:, None], tokens[token_ids], jnp.zeros((), jnp.bfloat16))
                row_grads = jnp.where(is_live[:, None], out_grad[token_ids], jnp.zeros((), jnp.bfloat16))
                row_probs = jnp.where(is_live, probs_flat[slot_ids], jnp.zeros((), jnp.bfloat16))
                slot_input, prob_grad, hidden, slot_grad, pre_gate, pre_up = slot_backward(
                    row_tokens, row_grads, row_probs, gate_mat, up_mat, down_mat)
                grad_acc = grad_acc.at[token_ids].add(
                    jnp.where(is_live[:, None], slot_input.astype(jnp.float32), jnp.zeros((), jnp.float32)))
                target = jnp.where(is_live, slot_ids, slot_count).astype(jnp.int32)
                prob_out = prob_out.at[target].set(prob_grad, mode="drop")
                part_gate = part_gate + contract_rows(row_tokens, pre_gate)
                part_up = part_up + contract_rows(row_tokens, pre_up)
                part_down = part_down + contract_rows(hidden, slot_grad)
                return grad_acc, prob_out, part_gate, part_up, part_down

            block_total = ((live_rows + block_rows - 1) // block_rows).astype(jnp.int32)
            state = (grad_acc, prob_out, jnp.zeros((D, FF), jnp.float32), jnp.zeros((D, FF), jnp.float32),
                     jnp.zeros((FF, D), jnp.float32))
            grad_acc, prob_out, part_gate, part_up, part_down = lax.fori_loop(0, block_total, block_step, state)
            rounded = lax.optimization_barrier((part_gate.astype(jnp.bfloat16), part_up.astype(jnp.bfloat16),
                                                part_down.astype(jnp.bfloat16)))
            return (grad_acc, prob_out, sum_gate + rounded[0].astype(jnp.float32),
                    sum_up + rounded[1].astype(jnp.float32), sum_down + rounded[2].astype(jnp.float32))

        inner = (grad_acc, prob_out, jnp.zeros((D, FF), jnp.float32), jnp.zeros((D, FF), jnp.float32),
                 jnp.zeros((FF, D), jnp.float32))
        grad_acc, prob_out, sum_gate, sum_up, sum_down = lax.fori_loop(0, REPLICAS, replica_step, inner)
        gate_out = gate_out.at[expert].set(sum_gate.astype(jnp.bfloat16))
        up_out = up_out.at[expert].set(sum_up.astype(jnp.bfloat16))
        down_out = down_out.at[expert].set(sum_down.astype(jnp.bfloat16))
        return grad_acc, prob_out, gate_out, up_out, down_out

    carry = (jnp.zeros((TOKENS, D), jnp.float32), jnp.zeros((slot_count,), jnp.float32),
             jnp.zeros((EXPERTS, D, FF), jnp.bfloat16), jnp.zeros((EXPERTS, D, FF), jnp.bfloat16),
             jnp.zeros((EXPERTS, FF, D), jnp.bfloat16))
    grad_acc, prob_out, gate_out, up_out, down_out = lax.fori_loop(0, EXPERTS, expert_step, carry)
    grad_tokens = grad_acc.astype(jnp.bfloat16)
    grad_probs = prob_out.reshape(TOKENS, TOPK).astype(jnp.bfloat16)
    return (grad_tokens, grad_probs, gate_out, up_out, down_out)
```

```python
import jax
import jax.numpy as jnp
from jax import lax
from jax.sharding import PartitionSpec as P


def contract_rows(left, right):
    return lax.dot_general(
        left, right, (((0,), (0,)), ((), ())), preferred_element_type=jnp.float32
    )


def contract_cols(left, right):
    return lax.dot_general(
        left, right, (((1,), (1,)), ((), ())), preferred_element_type=jnp.float32
    )


def slot_positions(keys, width):
    members = (keys[:, None] == jnp.arange(width, dtype=jnp.int32)[None, :]).astype(jnp.int32)
    earlier = jnp.cumsum(members, axis=0) - members
    return jnp.sum(earlier * members, axis=1)


def expert_backward(row_tokens, row_grads, row_probs, gate_mat, up_mat, down_mat):
    gate = jnp.dot(row_tokens, gate_mat, preferred_element_type=jnp.float32)
    up_value = jnp.dot(row_tokens, up_mat, preferred_element_type=jnp.float32)
    sigmoid_g = jax.nn.sigmoid(gate)
    active = gate * sigmoid_g
    hidden = (active * up_value).astype(jnp.bfloat16)
    expert_out = jnp.dot(hidden, down_mat, preferred_element_type=jnp.float32).astype(jnp.bfloat16)
    prob_grad = jnp.sum(
        row_grads.astype(jnp.float32) * expert_out.astype(jnp.float32), axis=1
    ).astype(jnp.bfloat16)
    slot_grad = (row_probs.astype(jnp.float32)[:, None] * row_grads.astype(jnp.float32)).astype(
        jnp.bfloat16
    )
    grad_hidden = contract_cols(slot_grad, down_mat)
    pre_gate = (grad_hidden * up_value * sigmoid_g * (1.0 + gate * (1.0 - sigmoid_g))).astype(
        jnp.bfloat16
    )
    pre_up = (grad_hidden * active).astype(jnp.bfloat16)
    slot_input = (contract_cols(pre_gate, gate_mat) + contract_cols(pre_up, up_mat)).astype(
        jnp.bfloat16
    )
    pre_both = jnp.concatenate([pre_gate, pre_up], axis=1)
    return (slot_input, prob_grad, hidden, slot_grad, pre_both)


def weight_grads(row_tokens, hidden, slot_grad, pre_both):
    hidden_units = hidden.shape[1]
    columns = row_tokens
    gate_up = lax.psum_scatter(
        contract_rows(columns, pre_both).astype(jnp.bfloat16),
        "rep",
        scatter_dimension=0,
        tiled=True,
    ).astype(jnp.float32)
    columns = hidden
    down_sum = lax.psum_scatter(
        contract_rows(columns, slot_grad).astype(jnp.bfloat16),
        "rep",
        scatter_dimension=0,
        tiled=True,
    )
    grad_gate = gate_up[:, :hidden_units].astype(jnp.bfloat16)[None]
    grad_up = gate_up[:, hidden_units:].astype(jnp.bfloat16)[None]
    return (grad_gate, grad_up, down_sum[None])


def body(tokens, out_grad, routes, route_probs, w_gate, w_up, w_down):
    tok_count = tokens.shape[0]
    model_width = tokens.shape[1]
    top_count = routes.shape[1]
    hot_rows = tok_count - tok_count // 8
    group_size = lax.axis_size("exp")
    group_total = lax.axis_size("grp")
    hot_cap = hot_rows * top_count // group_size
    cold_cap = (tok_count - hot_rows) * top_count // group_size
    chunk = hot_cap + (group_total - 1) * cold_cap
    gate_mat = w_gate[0]
    up_mat = w_up[0]
    down_mat = w_down[0]
    experts_held = group_total * group_size
    slot_expert = routes.reshape(-1)
    slot_group = slot_expert // group_size
    slot_local = slot_expert % group_size
    group_hits = jnp.sum(
        (slot_group[:, None] == jnp.arange(group_total, dtype=jnp.int32)[None, :]).astype(jnp.int32),
        axis=0,
    )
    hot_group = jnp.argmax(group_hits).astype(jnp.int32)
    rel = (slot_group - hot_group) % group_total
    group_offset = jnp.where(rel == 0, 0, hot_cap + (rel - 1) * cold_cap)
    slot_index = (
        slot_local * chunk + group_offset + slot_positions(slot_expert, experts_held)
    )
    both = jnp.concatenate([tokens, out_grad], axis=1)
    send_both = (
        jnp.zeros((group_size * chunk, 2 * model_width), jnp.bfloat16)
        .at[slot_index]
        .set(jnp.repeat(both, top_count, axis=0))
    )
    send_probs = (
        jnp.zeros((group_size * chunk,), jnp.bfloat16).at[slot_index].set(route_probs.reshape(-1))
    )
    got_both = lax.all_to_all(
        send_both.reshape(group_size, chunk, 2 * model_width), "exp", 0, 0, tiled=True
    )
    got_probs = lax.all_to_all(send_probs.reshape(group_size, chunk), "exp", 0, 0, tiled=True)
    all_both = lax.all_gather(got_both, "grp", axis=0, tiled=False)
    all_probs = lax.all_gather(got_probs, "grp", axis=0, tiled=False)
    my_rel = (lax.axis_index("grp") - hot_group) % group_total
    my_offset = jnp.where(my_rel == 0, 0, hot_cap + (my_rel - 1) * cold_cap)
    my_cap = jnp.where(my_rel == 0, hot_cap, cold_cap)
    pad_both = jnp.pad(all_both, ((0, 0), (0, 0), (0, hot_cap), (0, 0)))
    pad_probs = jnp.pad(all_probs, ((0, 0), (0, 0), (0, hot_cap)))
    sel_both = lax.dynamic_slice_in_dim(pad_both, my_offset, hot_cap, axis=2)
    sel_probs = lax.dynamic_slice_in_dim(pad_probs, my_offset, hot_cap, axis=2)
    live = (jnp.arange(hot_cap, dtype=jnp.int32) < my_cap)[None, None, :]
    sel_probs = jnp.where(live, sel_probs, jnp.zeros((), jnp.bfloat16))
    expert_rows = group_total * group_size * hot_cap
    sel_both = sel_both.reshape(expert_rows, 2 * model_width)
    row_tokens = sel_both[:, :model_width]
    row_grads = sel_both[:, model_width:]
    row_probs = sel_probs.reshape(expert_rows)
    slot_input, prob_grad, hidden, slot_grad, pre_both = expert_backward(
        row_tokens, row_grads, row_probs, gate_mat, up_mat, down_mat
    )
    prob_grad = jnp.where(live, prob_grad.reshape(group_total, group_size, hot_cap), 0)
    back_input = lax.dynamic_update_slice_in_dim(
        jnp.zeros((group_total, group_size, chunk + hot_cap, model_width), jnp.bfloat16),
        slot_input.reshape(group_total, group_size, hot_cap, model_width),
        my_offset,
        axis=2,
    )[:, :, :chunk]
    back_probs = lax.dynamic_update_slice_in_dim(
        jnp.zeros((group_total, group_size, chunk + hot_cap), jnp.bfloat16),
        prob_grad.astype(jnp.bfloat16),
        my_offset,
        axis=2,
    )[:, :, :chunk]
    mine_input = lax.psum_scatter(back_input, "grp", scatter_dimension=0, tiled=True)[0]
    mine_probs = lax.psum_scatter(back_probs, "grp", scatter_dimension=0, tiled=True)[0]
    ret_input = lax.all_to_all(mine_input, "exp", 0, 0, tiled=True)
    ret_probs = lax.all_to_all(mine_probs, "exp", 0, 0, tiled=True)
    slot_grads = ret_input.reshape(group_size * chunk, model_width)[slot_index]
    grad_tokens = jnp.sum(
        slot_grads.reshape(tok_count, top_count, model_width).astype(jnp.float32), axis=1
    ).astype(jnp.bfloat16)
    grad_probs = ret_probs.reshape(group_size * chunk)[slot_index].reshape(tok_count, top_count)
    grad_gate, grad_up, grad_down = weight_grads(row_tokens, hidden, slot_grad, pre_both)
    return (grad_tokens, grad_probs, grad_gate, grad_up, grad_down)


def solution(mesh):
    return jax.shard_map(
        body,
        mesh=mesh,
        in_specs=(
            P(("rep", "grp", "exp"), None),
            P(("rep", "grp", "exp"), None),
            P(("rep", "grp", "exp"), None),
            P(("rep", "grp", "exp"), None),
            P(("grp", "exp"), None, None),
            P(("grp", "exp"), None, None),
            P(("grp", "exp"), None, None),
        ),
        out_specs=(
            P(("rep", "grp", "exp"), None),
            P(("rep", "grp", "exp"), None),
            P(("grp", "exp"), "rep", None),
            P(("grp", "exp"), "rep", None),
            P(("grp", "exp"), "rep", None),
        ),
        check_vma=False,
    )
```

```python
import jax
import jax.numpy as jnp
from jax import lax
from jax.sharding import PartitionSpec as P


def contract_rows(left, right):
    return lax.dot_general(
        left, right, (((0,), (0,)), ((), ())), preferred_element_type=jnp.float32
    )


def contract_cols(left, right):
    return lax.dot_general(
        left, right, (((1,), (1,)), ((), ())), preferred_element_type=jnp.float32
    )


def slot_positions(keys, width):
    members = (keys[:, None] == jnp.arange(width, dtype=jnp.int32)[None, :]).astype(jnp.int32)
    earlier = jnp.cumsum(members, axis=0) - members
    return jnp.sum(earlier * members, axis=1)


def expert_backward(row_tokens, row_grads, row_probs, gate_mat, up_mat, down_mat):
    gate = jnp.dot(row_tokens, gate_mat, preferred_element_type=jnp.float32)
    up_value = jnp.dot(row_tokens, up_mat, preferred_element_type=jnp.float32)
    sigmoid_g = jax.nn.sigmoid(gate)
    active = gate * sigmoid_g
    hidden = (active * up_value).astype(jnp.bfloat16)
    expert_out = jnp.dot(hidden, down_mat, preferred_element_type=jnp.float32).astype(jnp.bfloat16)
    prob_grad = jnp.sum(
        row_grads.astype(jnp.float32) * expert_out.astype(jnp.float32), axis=1
    ).astype(jnp.bfloat16)
    slot_grad = (row_probs.astype(jnp.float32)[:, None] * row_grads.astype(jnp.float32)).astype(
        jnp.bfloat16
    )
    grad_hidden = contract_cols(slot_grad, down_mat)
    pre_gate = (grad_hidden * up_value * sigmoid_g * (1.0 + gate * (1.0 - sigmoid_g))).astype(
        jnp.bfloat16
    )
    pre_up = (grad_hidden * active).astype(jnp.bfloat16)
    slot_input = (contract_cols(pre_gate, gate_mat) + contract_cols(pre_up, up_mat)).astype(
        jnp.bfloat16
    )
    pre_both = jnp.concatenate([pre_gate, pre_up], axis=1)
    return (slot_input, prob_grad, hidden, slot_grad, pre_both)


def weight_grads(row_tokens, hidden, slot_grad, pre_both):
    hidden_units = hidden.shape[1]
    columns = row_tokens
    gate_up = lax.psum_scatter(
        contract_rows(columns, pre_both).astype(jnp.bfloat16),
        "rep",
        scatter_dimension=0,
        tiled=True,
    ).astype(jnp.float32)
    columns = hidden
    down_sum = lax.psum_scatter(
        contract_rows(columns, slot_grad).astype(jnp.bfloat16),
        "rep",
        scatter_dimension=0,
        tiled=True,
    )
    grad_gate = gate_up[:, :hidden_units].astype(jnp.bfloat16)[None]
    grad_up = gate_up[:, hidden_units:].astype(jnp.bfloat16)[None]
    return (grad_gate, grad_up, down_sum[None])


def body(tokens, out_grad, routes, route_probs, w_gate, w_up, w_down):
    tok_count = tokens.shape[0]
    model_width = tokens.shape[1]
    top_count = routes.shape[1]
    hot_rows = tok_count - tok_count // 8
    group_size = lax.axis_size("exp")
    group_total = lax.axis_size("grp")
    hot_cap = hot_rows * top_count // group_size
    cold_cap = (tok_count - hot_rows) * top_count // group_size
    chunk = hot_cap + (group_total - 1) * cold_cap
    gate_mat = w_gate[0]
    up_mat = w_up[0]
    down_mat = w_down[0]
    experts_held = group_total * group_size
    slot_expert = routes.reshape(-1)
    slot_group = slot_expert // group_size
    slot_local = slot_expert % group_size
    group_hits = jnp.sum(
        (slot_group[:, None] == jnp.arange(group_total, dtype=jnp.int32)[None, :]).astype(jnp.int32),
        axis=0,
    )
    hot_group = jnp.argmax(group_hits).astype(jnp.int32)
    rel = (slot_group - hot_group) % group_total
    group_offset = jnp.where(rel == 0, 0, hot_cap + (rel - 1) * cold_cap)
    slot_index = (
        slot_local * chunk + group_offset + slot_positions(slot_expert, experts_held)
    )
    send_tokens = (
        jnp.zeros((group_size * chunk, model_width), jnp.bfloat16)
        .at[slot_index]
        .set(jnp.repeat(tokens, top_count, axis=0))
    )
    send_grads = (
        jnp.zeros((group_size * chunk, model_width), jnp.bfloat16)
        .at[slot_index]
        .set(jnp.repeat(out_grad, top_count, axis=0))
    )
    send_probs = (
        jnp.zeros((group_size * chunk,), jnp.bfloat16).at[slot_index].set(route_probs.reshape(-1))
    )
    my_rel = (lax.axis_index("grp") - hot_group) % group_total
    my_offset = jnp.where(my_rel == 0, 0, hot_cap + (my_rel - 1) * cold_cap)
    my_cap = jnp.where(my_rel == 0, hot_cap, cold_cap)
    expert_rows = group_total * group_size * hot_cap

    def dispatch(send, tail):
        got = lax.all_to_all(send.reshape((group_size, chunk) + tail), "exp", 0, 0, tiled=True)
        gathered = lax.all_gather(got, "grp", axis=0, tiled=False)
        widths = ((0, 0), (0, 0), (0, hot_cap)) + ((0, 0),) * len(tail)
        return lax.dynamic_slice_in_dim(jnp.pad(gathered, widths), my_offset, hot_cap, axis=2)

    live = (jnp.arange(hot_cap, dtype=jnp.int32) < my_cap)[None, None, :]
    row_tokens = dispatch(send_tokens, (model_width,)).reshape(expert_rows, model_width)
    row_grads = dispatch(send_grads, (model_width,)).reshape(expert_rows, model_width)
    sel_probs = jnp.where(live, dispatch(send_probs, ()), jnp.zeros((), jnp.bfloat16))
    row_probs = sel_probs.reshape(expert_rows)
    slot_input, prob_grad, hidden, slot_grad, pre_both = expert_backward(
        row_tokens, row_grads, row_probs, gate_mat, up_mat, down_mat
    )
    prob_grad = jnp.where(live, prob_grad.reshape(group_total, group_size, hot_cap), 0)
    back_input = lax.dynamic_update_slice_in_dim(
        jnp.zeros((group_total, group_size, chunk + hot_cap, model_width), jnp.bfloat16),
        slot_input.reshape(group_total, group_size, hot_cap, model_width),
        my_offset,
        axis=2,
    )[:, :, :chunk]
    back_probs = lax.dynamic_update_slice_in_dim(
        jnp.zeros((group_total, group_size, chunk + hot_cap), jnp.bfloat16),
        prob_grad.astype(jnp.bfloat16),
        my_offset,
        axis=2,
    )[:, :, :chunk]
    mine_input = lax.psum_scatter(back_input, "grp", scatter_dimension=0, tiled=True)[0]
    mine_probs = lax.psum_scatter(back_probs, "grp", scatter_dimension=0, tiled=True)[0]
    ret_input = lax.all_to_all(mine_input, "exp", 0, 0, tiled=True)
    ret_probs = lax.all_to_all(mine_probs, "exp", 0, 0, tiled=True)
    slot_grads = ret_input.reshape(group_size * chunk, model_width)[slot_index]
    grad_tokens = jnp.sum(
        slot_grads.reshape(tok_count, top_count, model_width).astype(jnp.float32), axis=1
    ).astype(jnp.bfloat16)
    grad_probs = ret_probs.reshape(group_size * chunk)[slot_index].reshape(tok_count, top_count)
    grad_gate, grad_up, grad_down = weight_grads(row_tokens, hidden, slot_grad, pre_both)
    return (grad_tokens, grad_probs, grad_gate, grad_up, grad_down)


def solution(mesh):
    return jax.shard_map(
        body,
        mesh=mesh,
        in_specs=(
            P(("rep", "grp", "exp"), None),
            P(("rep", "grp", "exp"), None),
            P(("rep", "grp", "exp"), None),
            P(("rep", "grp", "exp"), None),
            P(("grp", "exp"), None, None),
            P(("grp", "exp"), None, None),
            P(("grp", "exp"), None, None),
        ),
        out_specs=(
            P(("rep", "grp", "exp"), None),
            P(("rep", "grp", "exp"), None),
            P(("grp", "exp"), "rep", None),
            P(("grp", "exp"), "rep", None),
            P(("grp", "exp"), "rep", None),
        ),
        check_vma=False,
    )
```

```python
import jax
import jax.numpy as jnp
from jax import lax
from jax.sharding import PartitionSpec as P


def contract_rows(left, right):
    return lax.dot_general(
        left, right, (((0,), (0,)), ((), ())), preferred_element_type=jnp.float32
    )


def contract_cols(left, right):
    return lax.dot_general(
        left, right, (((1,), (1,)), ((), ())), preferred_element_type=jnp.float32
    )


def slot_positions(keys, width):
    members = (keys[:, None] == jnp.arange(width, dtype=jnp.int32)[None, :]).astype(jnp.int32)
    earlier = jnp.cumsum(members, axis=0) - members
    return jnp.sum(earlier * members, axis=1)


def expert_backward(row_tokens, row_grads, row_probs, gate_mat, up_mat, down_mat):
    gate = jnp.dot(row_tokens, gate_mat, preferred_element_type=jnp.float32)
    up_value = jnp.dot(row_tokens, up_mat, preferred_element_type=jnp.float32)
    sigmoid_g = jax.nn.sigmoid(gate)
    active = gate * sigmoid_g
    hidden = (active * up_value).astype(jnp.bfloat16)
    expert_out = jnp.dot(hidden, down_mat, preferred_element_type=jnp.float32).astype(jnp.bfloat16)
    prob_grad = jnp.sum(
        row_grads.astype(jnp.float32) * expert_out.astype(jnp.float32), axis=1
    ).astype(jnp.bfloat16)
    slot_grad = (row_probs.astype(jnp.float32)[:, None] * row_grads.astype(jnp.float32)).astype(
        jnp.bfloat16
    )
    grad_hidden = contract_cols(slot_grad, down_mat)
    pre_gate = (grad_hidden * up_value * sigmoid_g * (1.0 + gate * (1.0 - sigmoid_g))).astype(
        jnp.bfloat16
    )
    pre_up = (grad_hidden * active).astype(jnp.bfloat16)
    slot_input = (contract_cols(pre_gate, gate_mat) + contract_cols(pre_up, up_mat)).astype(
        jnp.bfloat16
    )
    pre_both = jnp.concatenate([pre_gate, pre_up], axis=1)
    return (slot_input, prob_grad, hidden, slot_grad, pre_both)


def weight_grads(row_tokens, hidden, slot_grad, pre_both):
    hidden_units = hidden.shape[1]
    columns = row_tokens
    gate_up = lax.psum_scatter(
        contract_rows(columns, pre_both).astype(jnp.bfloat16),
        "rep",
        scatter_dimension=0,
        tiled=True,
    ).astype(jnp.float32)
    columns = hidden
    down_sum = lax.psum_scatter(
        contract_rows(columns, slot_grad).astype(jnp.bfloat16),
        "rep",
        scatter_dimension=0,
        tiled=True,
    )
    grad_gate = gate_up[:, :hidden_units].astype(jnp.bfloat16)[None]
    grad_up = gate_up[:, hidden_units:].astype(jnp.bfloat16)[None]
    return (grad_gate, grad_up, down_sum[None])


def body(tokens, out_grad, routes, route_probs, w_gate, w_up, w_down):
    tok_count = tokens.shape[0]
    model_width = tokens.shape[1]
    top_count = routes.shape[1]
    hot_rows = tok_count - tok_count // 8
    group_size = lax.axis_size("exp")
    group_total = lax.axis_size("grp")
    hot_cap = hot_rows * top_count // group_size
    cold_cap = (tok_count - hot_rows) * top_count // group_size
    chunk = hot_cap + (group_total - 1) * cold_cap
    gate_mat = w_gate[0]
    up_mat = w_up[0]
    down_mat = w_down[0]
    experts_held = group_total * group_size
    slot_expert = routes.reshape(-1)
    slot_group = slot_expert // group_size
    slot_local = slot_expert % group_size
    group_hits = jnp.sum(
        (slot_group[:, None] == jnp.arange(group_total, dtype=jnp.int32)[None, :]).astype(jnp.int32),
        axis=0,
    )
    hot_group = jnp.argmax(group_hits).astype(jnp.int32)
    rel = (slot_group - hot_group) % group_total
    group_offset = jnp.where(rel == 0, 0, hot_cap + (rel - 1) * cold_cap)
    slot_index = (
        slot_local * chunk + group_offset + slot_positions(slot_expert, experts_held)
    )
    my_rel = (lax.axis_index("grp") - hot_group) % group_total
    my_offset = jnp.where(my_rel == 0, 0, hot_cap + (my_rel - 1) * cold_cap)
    my_expert = lax.axis_index("grp") * group_size + lax.axis_index("exp")
    expert_rows = group_total * group_size * hot_cap
    sources = group_total * group_size

    def gather_all(x):
        return lax.all_gather(lax.all_gather(x, "exp", axis=0, tiled=False), "grp", axis=0, tiled=False)

    all_routes = gather_all(routes).reshape(sources, tok_count * top_count)
    all_probs = gather_all(route_probs).reshape(sources, tok_count * top_count)
    member = (all_routes == my_expert).astype(jnp.int32)
    place = jnp.cumsum(member, axis=1) - 1
    counts = jnp.sum(member, axis=1)
    place = jnp.where(member > 0, place, hot_cap)
    src_rows = jnp.arange(sources, dtype=jnp.int32)[:, None]
    slot_ids = jnp.broadcast_to(jnp.arange(tok_count * top_count, dtype=jnp.int32)[None, :], place.shape)
    picked = jnp.zeros((sources, hot_cap), jnp.int32).at[src_rows, place].set(slot_ids, mode="drop")
    live = jnp.arange(hot_cap, dtype=jnp.int32)[None, :] < counts[:, None]
    row_index = (src_rows * tok_count + picked // top_count).reshape(expert_rows)
    row_tokens = gather_all(tokens).reshape(sources * tok_count, model_width)[row_index]
    row_grads = gather_all(out_grad).reshape(sources * tok_count, model_width)[row_index]
    sel_probs = jnp.where(
        live, jnp.take_along_axis(all_probs, picked, axis=1), jnp.zeros((), jnp.bfloat16)
    )
    live = live.reshape(group_total, group_size, hot_cap)
    row_probs = sel_probs.reshape(expert_rows)
    slot_input, prob_grad, hidden, slot_grad, pre_both = expert_backward(
        row_tokens, row_grads, row_probs, gate_mat, up_mat, down_mat
    )
    prob_grad = jnp.where(live, prob_grad.reshape(group_total, group_size, hot_cap), 0)
    back_input = lax.dynamic_update_slice_in_dim(
        jnp.zeros((group_total, group_size, chunk + hot_cap, model_width), jnp.bfloat16),
        slot_input.reshape(group_total, group_size, hot_cap, model_width),
        my_offset,
        axis=2,
    )[:, :, :chunk]
    back_probs = lax.dynamic_update_slice_in_dim(
        jnp.zeros((group_total, group_size, chunk + hot_cap), jnp.bfloat16),
        prob_grad.astype(jnp.bfloat16),
        my_offset,
        axis=2,
    )[:, :, :chunk]
    mine_input = lax.psum_scatter(back_input, "grp", scatter_dimension=0, tiled=True)[0]
    mine_probs = lax.psum_scatter(back_probs, "grp", scatter_dimension=0, tiled=True)[0]
    ret_input = lax.all_to_all(mine_input, "exp", 0, 0, tiled=True)
    ret_probs = lax.all_to_all(mine_probs, "exp", 0, 0, tiled=True)
    slot_grads = ret_input.reshape(group_size * chunk, model_width)[slot_index]
    grad_tokens = jnp.sum(
        slot_grads.reshape(tok_count, top_count, model_width).astype(jnp.float32), axis=1
    ).astype(jnp.bfloat16)
    grad_probs = ret_probs.reshape(group_size * chunk)[slot_index].reshape(tok_count, top_count)
    grad_gate, grad_up, grad_down = weight_grads(row_tokens, hidden, slot_grad, pre_both)
    return (grad_tokens, grad_probs, grad_gate, grad_up, grad_down)


def solution(mesh):
    return jax.shard_map(
        body,
        mesh=mesh,
        in_specs=(
            P(("rep", "grp", "exp"), None),
            P(("rep", "grp", "exp"), None),
            P(("rep", "grp", "exp"), None),
            P(("rep", "grp", "exp"), None),
            P(("grp", "exp"), None, None),
            P(("grp", "exp"), None, None),
            P(("grp", "exp"), None, None),
        ),
        out_specs=(
            P(("rep", "grp", "exp"), None),
            P(("rep", "grp", "exp"), None),
            P(("grp", "exp"), "rep", None),
            P(("grp", "exp"), "rep", None),
            P(("grp", "exp"), "rep", None),
        ),
        check_vma=False,
    )
```

```python
import jax
import jax.numpy as jnp
from jax import lax
from jax.sharding import PartitionSpec as P


def contract_rows(left, right):
    return lax.dot_general(
        left, right, (((0,), (0,)), ((), ())), preferred_element_type=jnp.float32
    )


def contract_cols(left, right):
    return lax.dot_general(
        left, right, (((1,), (1,)), ((), ())), preferred_element_type=jnp.float32
    )


def slot_positions(keys, width):
    members = (keys[:, None] == jnp.arange(width, dtype=jnp.int32)[None, :]).astype(jnp.int32)
    earlier = jnp.cumsum(members, axis=0) - members
    return jnp.sum(earlier * members, axis=1)


def expert_backward(row_tokens, row_grads, row_probs, gate_mat, up_mat, down_mat):
    gate = jnp.dot(row_tokens, gate_mat, preferred_element_type=jnp.float32)
    up_value = jnp.dot(row_tokens, up_mat, preferred_element_type=jnp.float32)
    sigmoid_g = jax.nn.sigmoid(gate)
    active = gate * sigmoid_g
    hidden = (active * up_value).astype(jnp.bfloat16)
    expert_out = jnp.dot(hidden, down_mat, preferred_element_type=jnp.float32).astype(jnp.bfloat16)
    prob_grad = jnp.sum(
        row_grads.astype(jnp.float32) * expert_out.astype(jnp.float32), axis=1
    ).astype(jnp.bfloat16)
    slot_grad = (row_probs.astype(jnp.float32)[:, None] * row_grads.astype(jnp.float32)).astype(
        jnp.bfloat16
    )
    grad_hidden = contract_cols(slot_grad, down_mat)
    pre_gate = (grad_hidden * up_value * sigmoid_g * (1.0 + gate * (1.0 - sigmoid_g))).astype(
        jnp.bfloat16
    )
    pre_up = (grad_hidden * active).astype(jnp.bfloat16)
    slot_input = (contract_cols(pre_gate, gate_mat) + contract_cols(pre_up, up_mat)).astype(
        jnp.bfloat16
    )
    pre_both = jnp.concatenate([pre_gate, pre_up], axis=1)
    return (slot_input, prob_grad, hidden, slot_grad, pre_both)


def weight_grads(row_tokens, hidden, slot_grad, pre_both):
    hidden_units = hidden.shape[1]
    columns = row_tokens
    gate_up = lax.psum_scatter(
        contract_rows(columns, pre_both).astype(jnp.bfloat16),
        "rep",
        scatter_dimension=0,
        tiled=True,
    ).astype(jnp.float32)
    columns = hidden
    down_sum = lax.psum_scatter(
        contract_rows(columns, slot_grad).astype(jnp.bfloat16),
        "rep",
        scatter_dimension=0,
        tiled=True,
    )
    grad_gate = gate_up[:, :hidden_units].astype(jnp.bfloat16)[None]
    grad_up = gate_up[:, hidden_units:].astype(jnp.bfloat16)[None]
    return (grad_gate, grad_up, down_sum[None])


def body(tokens, out_grad, routes, route_probs, w_gate, w_up, w_down):
    tok_count = tokens.shape[0]
    model_width = tokens.shape[1]
    top_count = routes.shape[1]
    hot_rows = tok_count - tok_count // 8
    group_size = lax.axis_size("exp")
    group_total = lax.axis_size("grp")
    hot_cap = hot_rows * top_count // group_size
    cold_cap = (tok_count - hot_rows) * top_count // group_size
    chunk = hot_cap + (group_total - 1) * cold_cap
    gate_mat = w_gate[0]
    up_mat = w_up[0]
    down_mat = w_down[0]
    experts_held = group_total * group_size
    slot_expert = routes.reshape(-1)
    slot_group = slot_expert // group_size
    slot_local = slot_expert % group_size
    group_hits = jnp.sum(
        (slot_group[:, None] == jnp.arange(group_total, dtype=jnp.int32)[None, :]).astype(jnp.int32),
        axis=0,
    )
    hot_group = jnp.argmax(group_hits).astype(jnp.int32)
    rel = (slot_group - hot_group) % group_total
    group_offset = jnp.where(rel == 0, 0, hot_cap + (rel - 1) * cold_cap)
    slot_index = (
        slot_local * chunk + group_offset + slot_positions(slot_expert, experts_held)
    )
    prob_band = jnp.zeros((tok_count, top_count, 128), jnp.bfloat16).at[:, :, 0].set(route_probs)
    both = jnp.concatenate(
        [jnp.repeat(jnp.concatenate([tokens, out_grad], axis=1), top_count, axis=0),
         prob_band.reshape(tok_count * top_count, 128)],
        axis=1,
    )
    send_both = (
        jnp.zeros((group_size * chunk, 2 * model_width + 128), jnp.bfloat16)
        .at[slot_index]
        .set(both)
    )
    got_both = lax.all_to_all(
        send_both.reshape(group_size, chunk, 2 * model_width + 128), "exp", 0, 0, tiled=True
    )
    all_both = lax.all_gather(got_both, "grp", axis=0, tiled=False)
    my_rel = (lax.axis_index("grp") - hot_group) % group_total
    my_offset = jnp.where(my_rel == 0, 0, hot_cap + (my_rel - 1) * cold_cap)
    my_cap = jnp.where(my_rel == 0, hot_cap, cold_cap)
    pad_both = jnp.pad(all_both, ((0, 0), (0, 0), (0, hot_cap), (0, 0)))
    sel_both = lax.dynamic_slice_in_dim(pad_both, my_offset, hot_cap, axis=2)
    sel_probs = sel_both[:, :, :, 2 * model_width]
    live = (jnp.arange(hot_cap, dtype=jnp.int32) < my_cap)[None, None, :]
    sel_probs = jnp.where(live, sel_probs, jnp.zeros((), jnp.bfloat16))
    expert_rows = group_total * group_size * hot_cap
    sel_both = sel_both.reshape(expert_rows, 2 * model_width + 128)
    row_tokens = sel_both[:, :model_width]
    row_grads = sel_both[:, model_width : 2 * model_width]
    row_probs = sel_probs.reshape(expert_rows)
    slot_input, prob_grad, hidden, slot_grad, pre_both = expert_backward(
        row_tokens, row_grads, row_probs, gate_mat, up_mat, down_mat
    )
    prob_grad = jnp.where(live, prob_grad.reshape(group_total, group_size, hot_cap), 0)
    back_input = lax.dynamic_update_slice_in_dim(
        jnp.zeros((group_total, group_size, chunk + hot_cap, model_width), jnp.bfloat16),
        slot_input.reshape(group_total, group_size, hot_cap, model_width),
        my_offset,
        axis=2,
    )[:, :, :chunk]
    back_probs = lax.dynamic_update_slice_in_dim(
        jnp.zeros((group_total, group_size, chunk + hot_cap), jnp.bfloat16),
        prob_grad.astype(jnp.bfloat16),
        my_offset,
        axis=2,
    )[:, :, :chunk]
    mine_input = lax.psum_scatter(back_input, "grp", scatter_dimension=0, tiled=True)[0]
    mine_probs = lax.psum_scatter(back_probs, "grp", scatter_dimension=0, tiled=True)[0]
    ret_input = lax.all_to_all(mine_input, "exp", 0, 0, tiled=True)
    ret_probs = lax.all_to_all(mine_probs, "exp", 0, 0, tiled=True)
    slot_grads = ret_input.reshape(group_size * chunk, model_width)[slot_index]
    grad_tokens = jnp.sum(
        slot_grads.reshape(tok_count, top_count, model_width).astype(jnp.float32), axis=1
    ).astype(jnp.bfloat16)
    grad_probs = ret_probs.reshape(group_size * chunk)[slot_index].reshape(tok_count, top_count)
    grad_gate, grad_up, grad_down = weight_grads(row_tokens, hidden, slot_grad, pre_both)
    return (grad_tokens, grad_probs, grad_gate, grad_up, grad_down)


def solution(mesh):
    return jax.shard_map(
        body,
        mesh=mesh,
        in_specs=(
            P(("rep", "grp", "exp"), None),
            P(("rep", "grp", "exp"), None),
            P(("rep", "grp", "exp"), None),
            P(("rep", "grp", "exp"), None),
            P(("grp", "exp"), None, None),
            P(("grp", "exp"), None, None),
            P(("grp", "exp"), None, None),
        ),
        out_specs=(
            P(("rep", "grp", "exp"), None),
            P(("rep", "grp", "exp"), None),
            P(("grp", "exp"), "rep", None),
            P(("grp", "exp"), "rep", None),
            P(("grp", "exp"), "rep", None),
        ),
        check_vma=False,
    )
```
